32 devices in a mesh: ma: 4 (over y, core), row: 8 (over z, x).
Axes of the slice: x: 2, y: 2, z: 4, core: 2. Of those that a mesh axis runs over, the one named last changes fastest.
Arguments:
- grid_fields: bfloat16 [4, 16, 1536, 2048], P(None, 'row', 'ma'), may hold values from -6 to 6
- pair_list: int32 [256], replicated, may hold values from 0 to 255, each once
- legendre: bfloat16 [256, 768, 1024], P(('ma', 'row')), may hold values from -0.21875 to 0.21875
- stencil_start: int32 [16], replicated, may hold values from 0 to 11, as said below
- first_weights: float32 [16, 5], replicated, may hold values from -6 to 6
- second_weights: float32 [16, 5], replicated, may hold values from -6 to 6
- inv_radius: float32 [16], replicated, may hold values from 1 to 2.86
Outputs:
- current: bfloat16 [3, 2, 256, 16, 1024], P(None, None, ('ma', 'row'))
- vorticity: bfloat16 [3, 2, 256, 16, 1024], P(None, None, ('ma', 'row'))
The draws below stay inside these ranges and needn't reach their ends.
Inputs may be any that keep to these rules, and one draw needn't show every extreme that they name: Every radius r lies inside its own stencil: stencil_start[r] <= r <= stencil_start[r] + 4.
All inputs are finite; a program needn't handle non-finite values.
Results may differ from the reference program's by a relative error of at most 0.0072.
Values may be sent and summed in bfloat16 or wider, within the bound.
A program may use at most 192 MiB of HBM per device.

```python
import math
import jax
import jax.numpy as jnp
from jax import lax

L = 1024
NLAT = 1536
NLON = 2048
PAIRS = 256
POT = 4
STEN = 5
R = 16


def draw_stencil_start(key, part):
    offsets = jax.random.randint(key, (R,), 0, STEN)
    return jnp.clip(jnp.arange(R) - offsets, 0, R - STEN).astype(jnp.int32)


def shard_levels(own_key, dims, pieces, low, top_value):
    def one(dim, blocks):
        draws = jax.random.uniform(jax.random.fold_in(jax.random.fold_in(own_key, 6), dim), (blocks,), jnp.float32, low / len(pieces), top_value / len(pieces))
        return jnp.repeat(jnp.exp(draws), dims[dim] // blocks).reshape((-1,) + (1,) * (len(dims) - dim - 1))

    loudness = one(*pieces[0])
    for cut in pieces[1:]:
        loudness = loudness * one(*cut)
    return loudness


def scatter_about(key, dims, deviation, limit, shards=(), held_as=jnp.bfloat16):
    result = deviation * jax.random.normal(key, dims, jnp.float32)
    if shards:
        result = result * shard_levels(key, dims, shards, -0.22, 0.18)
    return jnp.clip(result, -limit, limit).astype(held_as)


def setup_inputs(seed: int = 0) -> dict:
    keys = jax.random.split(jax.random.key(seed), 8)
    grid_fields = scatter_about(keys[0], (POT, R, NLAT, NLON), 1.0, 6.0, ((1, 8), (2, 4)))
    pair_list = jax.random.permutation(keys[1], PAIRS).astype(jnp.int32)
    legendre = scatter_about(keys[2], (PAIRS, NLAT // 2, L), (NLAT // 2) ** -0.5, 0.21875, ((0, 32),))
    stencil_start = draw_stencil_start(jax.random.fold_in(keys[7], 71), 0)
    first_weights = scatter_about(keys[4], (R, STEN), 1.0, 6.0, (), jnp.float32)
    second_weights = scatter_about(keys[5], (R, STEN), 1.0, 6.0, (), jnp.float32)
    inv_radius = jnp.clip(jnp.exp(jax.random.uniform(keys[6], (R,), jnp.float32, math.log(1.0), math.log(2.86))), 1.0, 2.86)
    return {"grid_fields": grid_fields, "pair_list": pair_list, "legendre": legendre, "stencil_start": stencil_start, "first_weights": first_weights, "second_weights": second_weights, "inv_radius": inv_radius}


def degree_table(pair_values, degrees):
    column = jnp.arange(degrees, dtype=jnp.int32)
    upper_side = column[None, :] >= (degrees - pair_values)[:, None]
    degree = jnp.where(upper_side, column[None, :], pair_values[:, None] + column[None, :])
    order_value = jnp.where(upper_side, degrees - pair_values[:, None], pair_values[:, None])
    parity = (degree - order_value) % 2
    return (upper_side.astype(jnp.int32), parity, degree)

def fourier_table(pair_values, degrees, points):
    orders = jnp.stack([pair_values, degrees - pair_values], axis=1)
    longitude = jnp.arange(points, dtype=jnp.int32)
    phases = orders[None, :, :] * longitude[:, None, None] % points
    angles = phases.astype(jnp.float32) * (2.0 * math.pi / points)
    factor = 1.0 / math.sqrt(points)
    return jnp.stack([jnp.cos(angles) * factor, -jnp.sin(angles) * factor], axis=-1).astype(jnp.bfloat16)

def derivative_matrix(stencil_start, weights):
    radius_count, stencil_width = weights.shape
    target = stencil_start[:, None] + jnp.arange(stencil_width, dtype=jnp.int32)[None, :]
    matches = target[:, :, None] == jnp.arange(radius_count, dtype=jnp.int32)[None, None, :]
    return lax.optimization_barrier(jnp.sum(jnp.where(matches, weights[:, :, None], 0.0), axis=1))

def radial(matrix, values):
    return jnp.einsum('rt,cjtk->cjrk', matrix, values, precision=lax.Precision.HIGHEST)

def curl_parts(poloidal, toroidal, first_matrix, second_matrix, horizontal, inverse):
    poloidal_first = radial(first_matrix, poloidal)
    poloidal_second = radial(second_matrix, poloidal)
    toroidal_first = radial(first_matrix, toroidal)
    radial_part = horizontal * inverse * toroidal
    spheroidal = toroidal_first + inverse * toroidal
    toroidal_part = -(poloidal_second + 2.0 * inverse * poloidal_first) + horizontal * inverse * inverse * poloidal
    return jnp.stack([radial_part, spheroidal, toroidal_part], axis=0).astype(jnp.bfloat16)

def reference(grid_fields, pair_list, legendre, stencil_start, first_weights, second_weights, inv_radius):
    fourier = fourier_table(pair_list, L, NLON).reshape(NLON, PAIRS * 4)

    def analyse(radius_index):
        one_radius = lax.dynamic_index_in_dim(grid_fields, radius_index, 1, False)
        flat = one_radius.reshape(POT * NLAT, NLON)
        values = jnp.dot(flat, fourier, preferred_element_type=jnp.float32)
        return values.astype(jnp.bfloat16).reshape(POT, NLAT, PAIRS, 2, 2)
    coefficients = lax.map(analyse, jnp.arange(R, dtype=jnp.int32))
    upper_side, parity, degree = degree_table(pair_list, L)
    two_values = jnp.arange(2, dtype=jnp.int32)

    def per_slot(slot_index):
        portion = lax.dynamic_index_in_dim(coefficients, slot_index, 3, False).astype(jnp.float32)
        northern = portion[:, :, :NLAT // 2]
        southern = jnp.flip(portion[:, :, NLAT // 2:], axis=2)
        folded = jnp.stack([northern + southern, northern - southern], axis=0).astype(jnp.bfloat16)
        matrix_block = jnp.moveaxis(folded, 3, 0).reshape(NLAT // 2, 2 * R * POT * 4)
        table_rows = lax.dynamic_index_in_dim(legendre, slot_index, 0, False)
        product = jnp.dot(matrix_block.T, table_rows, preferred_element_type=jnp.float32)
        product = product.reshape(2, R, POT, 2, 2, L)
        slot_parity = lax.dynamic_index_in_dim(parity, slot_index, 0, False)
        slot_side = lax.dynamic_index_in_dim(upper_side, slot_index, 0, False)
        selector = ((slot_parity[None, None, :] == two_values[:, None, None]) & (slot_side[None, None, :] == two_values[None, :, None])).astype(jnp.float32)
        chosen = lax.optimization_barrier(jnp.sum(product * selector[:, None, None, :, None, :], axis=(0, 3)))
        return jnp.transpose(chosen, (1, 2, 0, 3)).astype(jnp.bfloat16)
    spectral = jnp.transpose(lax.map(per_slot, jnp.arange(PAIRS, dtype=jnp.int32)), (1, 2, 0, 3, 4))
    first_matrix = derivative_matrix(stencil_start, first_weights)
    second_matrix = derivative_matrix(stencil_start, second_weights)
    horizontal = ((degree * (degree + 1)).astype(jnp.float32) / (L * L))[None, :, None, :]
    inverse = inv_radius[:, None]
    current = curl_parts(spectral[0].astype(jnp.float32), spectral[1].astype(jnp.float32), first_matrix, second_matrix, horizontal, inverse)
    vorticity = curl_parts(spectral[2].astype(jnp.float32), spectral[3].astype(jnp.float32), first_matrix, second_matrix, horizontal, inverse)
    return (current, vorticity)
```

```python
import math

import jax
import jax.numpy as jnp
from jax import lax
from jax.sharding import PartitionSpec as P


def degree_table(pair_values, degrees):
    column = jnp.arange(degrees, dtype=jnp.int32)
    upper_side = column[None, :] >= (degrees - pair_values)[:, None]
    degree = jnp.where(upper_side, column[None, :], pair_values[:, None] + column[None, :])
    order_value = jnp.where(upper_side, degrees - pair_values[:, None], pair_values[:, None])
    parity = (degree - order_value) % 2
    return (upper_side.astype(jnp.int32), parity, degree)


def fourier_table(pair_values, degrees, points):
    orders = jnp.stack([pair_values, degrees - pair_values], axis=1)
    stride = 128
    factor = 1.0 / math.sqrt(points)

    def waves(positions):
        phases = orders[:, :, None] * positions[None, None, :] % points
        angles = phases.astype(jnp.float32) * (2.0 * math.pi / points)
        return jnp.cos(angles), jnp.sin(angles)

    wide_cos, wide_sin = waves(jnp.arange(points // stride, dtype=jnp.int32) * stride)
    fine_cos, fine_sin = waves(jnp.arange(stride, dtype=jnp.int32))
    wide_cos, wide_sin = wide_cos[..., None] * factor, wide_sin[..., None] * factor
    fine_cos, fine_sin = fine_cos[:, :, None, :], fine_sin[:, :, None, :]
    cosine = wide_cos * fine_cos - wide_sin * fine_sin
    sine = wide_sin * fine_cos + wide_cos * fine_sin
    table = jnp.stack([cosine, -sine], axis=2).astype(jnp.bfloat16)
    return table.reshape(pair_values.shape[0], 4, points)


def derivative_matrix(stencil_start, weights):
    radius_count, stencil_width = weights.shape
    target = stencil_start[:, None] + jnp.arange(stencil_width, dtype=jnp.int32)[None, :]
    matches = target[:, :, None] == jnp.arange(radius_count, dtype=jnp.int32)[None, None, :]
    return jnp.sum(jnp.where(matches, weights[:, :, None], 0.0), axis=1)


def radial(matrix, values):
    return jnp.einsum("rt,cjtk->cjrk", matrix, values, precision=lax.Precision.HIGHEST)


def curl_parts(poloidal, toroidal, first_matrix, second_matrix, horizontal, inverse):
    poloidal_first = radial(first_matrix, poloidal)
    poloidal_second = radial(second_matrix, poloidal)
    toroidal_first = radial(first_matrix, toroidal)
    radial_part = horizontal * inverse * toroidal
    spheroidal = toroidal_first + inverse * toroidal
    toroidal_part = (
        -(poloidal_second + 2.0 * inverse * poloidal_first)
        + horizontal * inverse * inverse * poloidal
    )
    return jnp.stack([radial_part, spheroidal, toroidal_part], axis=0).astype(jnp.bfloat16)


def select_columns(product, pair_values, degrees):
    upper_side, parity, _ = degree_table(pair_values, degrees)
    wide = (slice(None),) + (None,) * 3 + (slice(None),)
    by_side = jnp.where(upper_side[:, None][wide] == 1, product[:, :, 1], product[:, :, 0])
    return jnp.where(parity[wide] == 1, by_side[:, 1], by_side[:, 0])


def shards(
    grid_fields, pair_list, legendre, stencil_start, first_weights, second_weights, inv_radius
):
    potentials, rad_local, lat_local, points = grid_fields.shape
    degrees = legendre.shape[2]
    slots_here = legendre.shape[0]
    band_count = lax.axis_size("ma")
    rows_axis = lax.axis_size("row")
    fourier = fourier_table(pair_list, degrees, points)
    coefficients = jnp.einsum(
        "jsx,prhx->jsprh", fourier, grid_fields, preferred_element_type=jnp.float32
    ).astype(jnp.bfloat16)
    southern = lax.axis_index("ma") >= band_count // 2
    coefficients = jnp.where(southern, jnp.flip(coefficients, axis=-1), coefficients)
    at_owners = lax.all_to_all(
        coefficients, ("ma", "row"), split_axis=0, concat_axis=0, tiled=True
    ).reshape(band_count, rows_axis, slots_here, 2, 2, potentials, rad_local, lat_local)
    first_slot = (lax.axis_index("ma") * rows_axis + lax.axis_index("row")) * slots_here
    own_pairs = lax.dynamic_slice_in_dim(pair_list, first_slot, slots_here, 0)
    widened = at_owners.astype(jnp.float32)
    north = widened[: band_count // 2]
    south = jnp.flip(widened[band_count // 2 :], axis=0)
    folded = jnp.stack([north + south, north - south], axis=0).astype(jnp.bfloat16)
    folded = jnp.transpose(folded, (3, 0, 4, 5, 6, 2, 7, 1, 8)).reshape(
        slots_here, 8 * potentials * rows_axis * rad_local, -1
    )
    product = jnp.einsum("jmh,jhk->jmk", folded, legendre, preferred_element_type=jnp.float32)
    product = product.reshape(slots_here, 2, 2, 2, potentials, rows_axis * rad_local, degrees)
    chosen = select_columns(product, own_pairs, degrees).astype(jnp.bfloat16)
    spectral = jnp.transpose(chosen, (2, 1, 0, 3, 4))
    degree = degree_table(own_pairs, degrees)[2]
    horizontal = ((degree * (degree + 1)).astype(jnp.float32) / (degrees * degrees))[
        None, :, None, :
    ]
    inverse = inv_radius[:, None]
    first_matrix = derivative_matrix(stencil_start, first_weights)
    second_matrix = derivative_matrix(stencil_start, second_weights)
    widened = spectral.astype(jnp.float32)
    current = curl_parts(widened[0], widened[1], first_matrix, second_matrix, horizontal, inverse)
    vorticity = curl_parts(widened[2], widened[3], first_matrix, second_matrix, horizontal, inverse)
    return (current, vorticity)


def solution(mesh):
    in_specs = (P(None, "row", "ma", None), P(), P(("ma", "row"), None, None), P(), P(), P(), P())
    out_specs = (P(None, None, ("ma", "row"), None, None), P(None, None, ("ma", "row"), None, None))
    return jax.shard_map(shards, mesh=mesh, in_specs=in_specs, out_specs=out_specs, check_vma=False)
```

```python
import functools
import math

import jax
import jax.numpy as jnp
from jax import lax
from jax.experimental import pallas as pl
from jax.experimental.pallas import tpu as pltpu
from jax.sharding import PartitionSpec as P


def degree_table(pair_values, degrees):
    column = jnp.arange(degrees, dtype=jnp.int32)
    upper_side = column[None, :] >= (degrees - pair_values)[:, None]
    degree = jnp.where(upper_side, column[None, :], pair_values[:, None] + column[None, :])
    order_value = jnp.where(upper_side, degrees - pair_values[:, None], pair_values[:, None])
    parity = (degree - order_value) % 2
    return (upper_side.astype(jnp.int32), parity, degree)


def fourier_table(pair_values, degrees, points):
    orders = jnp.stack([pair_values, degrees - pair_values], axis=1)
    stride = 128
    factor = 1.0 / math.sqrt(points)

    def waves(positions):
        phases = orders[:, :, None] * positions[None, None, :] % points
        angles = phases.astype(jnp.float32) * (2.0 * math.pi / points)
        return jnp.cos(angles), jnp.sin(angles)

    wide_cos, wide_sin = waves(jnp.arange(points // stride, dtype=jnp.int32) * stride)
    fine_cos, fine_sin = waves(jnp.arange(stride, dtype=jnp.int32))
    wide_cos, wide_sin = wide_cos[..., None] * factor, wide_sin[..., None] * factor
    fine_cos, fine_sin = fine_cos[:, :, None, :], fine_sin[:, :, None, :]
    cosine = wide_cos * fine_cos - wide_sin * fine_sin
    sine = wide_sin * fine_cos + wide_cos * fine_sin
    table = jnp.stack([cosine, -sine], axis=2).astype(jnp.bfloat16)
    return table.reshape(pair_values.shape[0], 4, points)


def derivative_matrix(stencil_start, weights):
    radius_count, stencil_width = weights.shape
    target = stencil_start[:, None] + jnp.arange(stencil_width, dtype=jnp.int32)[None, :]
    matches = target[:, :, None] == jnp.arange(radius_count, dtype=jnp.int32)[None, None, :]
    return jnp.sum(jnp.where(matches, weights[:, :, None], 0.0), axis=1)


def radial(matrix, values):
    return jnp.einsum("rt,cjtk->cjrk", matrix, values, precision=lax.Precision.HIGHEST)


def curl_parts(poloidal, toroidal, first_matrix, second_matrix, horizontal, inverse):
    poloidal_first = radial(first_matrix, poloidal)
    poloidal_second = radial(second_matrix, poloidal)
    toroidal_first = radial(first_matrix, toroidal)
    radial_part = horizontal * inverse * toroidal
    spheroidal = toroidal_first + inverse * toroidal
    toroidal_part = (
        -(poloidal_second + 2.0 * inverse * poloidal_first)
        + horizontal * inverse * inverse * poloidal
    )
    return jnp.stack([radial_part, spheroidal, toroidal_part], axis=0).astype(jnp.bfloat16)


def select_columns(product, pair_values, degrees):
    upper_side, parity, _ = degree_table(pair_values, degrees)
    wide = (slice(None),) + (None,) * 3 + (slice(None),)
    by_side = jnp.where(upper_side[:, None][wide] == 1, product[:, :, 1], product[:, :, 0])
    return jnp.where(parity[wide] == 1, by_side[:, 1], by_side[:, 0])


def curl_matrix(stencil_start, first_weights, second_weights, inv_radius, potentials, groups):
    radii = inv_radius.shape[0]
    first = derivative_matrix(stencil_start, first_weights)
    second = derivative_matrix(stencil_start, second_weights)
    inverse = inv_radius[:, None]
    unit = jnp.eye(radii, dtype=jnp.float32)
    zero = jnp.zeros((radii, radii), jnp.float32)
    on_poloidal = [zero, zero, -(second + 2.0 * inverse * first), inverse * inverse * unit]
    on_toroidal = [inverse * unit, first + inverse * unit, zero, zero]
    pair_map = jnp.stack([jnp.stack(on_poloidal), jnp.stack(on_toroidal)])
    fields = potentials // 2
    whole = jnp.einsum("fe,pkrt->fkrept", jnp.eye(fields, dtype=jnp.float32), pair_map,
                       precision=lax.Precision.HIGHEST)
    whole = whole.reshape(fields * 4 * radii, potentials, groups, radii // groups)
    return jnp.transpose(whole, (0, 2, 1, 3)).reshape(fields * 4 * radii, potentials * radii)


def legendre_kernel(base, series, lat, degrees, pairs_ref, recv_ref, leg_ref, map_ref, *refs):
    cur_ref, vor_ref, lhs_ref = refs[-3:]
    bands, groups, rows = recv_ref.shape[:3]
    blocks = groups * series
    step = pl.program_id(0)

    @pl.when(step == 0)
    def _():
        flip = (
            lax.broadcasted_iota(jnp.int32, (lat, lat), 0)
            + lax.broadcasted_iota(jnp.int32, (lat, lat), 1)
            == lat - 1
        ).astype(jnp.bfloat16)
        total = blocks * rows
        out_row = lax.broadcasted_iota(jnp.int32, (total, total), 0)
        in_row = lax.broadcasted_iota(jnp.int32, (total, total), 1)
        wanted = (out_row % blocks) * rows + out_row // blocks
        order = (in_row == wanted).astype(jnp.bfloat16)

        def gathered(band):
            pieces = []
            for group in range(groups):
                values = recv_ref[band, group].astype(jnp.float32)
                pieces += [values[:, n * lat : (n + 1) * lat] for n in range(series)]
            return jnp.concatenate(pieces, axis=0)

        for band in range(bands // 2):
            north = gathered(band)
            south = gathered(bands - 1 - band).astype(jnp.bfloat16)
            south = jnp.dot(south, flip, preferred_element_type=jnp.float32)
            for parity, folded in enumerate((north + south, north - south)):
                sorted_rows = jnp.dot(
                    order, folded.astype(jnp.bfloat16), preferred_element_type=jnp.float32
                ).astype(jnp.bfloat16)
                for slot in range(rows // 4):
                    lhs_ref[slot, parity, :, band * lat : (band + 1) * lat] = sorted_rows[
                        slot * 4 * blocks : (slot + 1) * 4 * blocks
                    ]

    q = pairs_ref[base + step]
    width = 256
    for start in range(0, degrees, width):
        columns = slice(start, start + width)
        column = lax.broadcasted_iota(jnp.int32, (1, width), 1) + start
        upper = column >= degrees - q
        degree = jnp.where(upper, column, q + column)
        odd = ((degree - jnp.where(upper, degrees - q, q)) & 1) == 1
        horizontal = (degree * (degree + 1)).astype(jnp.float32) / (degrees * degrees)
        table = leg_ref[0, :, columns]
        even_part, odd_part = [
            jnp.dot(lhs_ref[step, parity], table, preferred_element_type=jnp.float32)
            for parity in range(2)
        ]
        chosen = jnp.where(odd, odd_part, even_part)
        chosen = jnp.where(upper, chosen[2 * blocks :], chosen[: 2 * blocks])
        chosen = chosen.astype(jnp.bfloat16).astype(jnp.float32)
        for part in range(2):
            results = jnp.dot(
                map_ref[...],
                chosen[part * blocks : (part + 1) * blocks],
                precision=lax.Precision.HIGHEST,
                preferred_element_type=jnp.float32,
            )
            radii = cur_ref.shape[3]
            for field, out_ref in enumerate((cur_ref, vor_ref)):
                kinds = [
                    results[(field * 4 + kind) * radii : (field * 4 + kind + 1) * radii]
                    for kind in range(4)
                ]
                out_ref[0, part, 0, :, columns] = (horizontal * kinds[0]).astype(jnp.bfloat16)
                out_ref[1, part, 0, :, columns] = kinds[1].astype(jnp.bfloat16)
                out_ref[2, part, 0, :, columns] = (kinds[2] + horizontal * kinds[3]).astype(
                    jnp.bfloat16
                )


def legendre_stage(base, received, legendre, own_pairs, curl_map, before, series, lat):
    bands, groups, rows, _ = received.shape
    slots_here, heights, degrees = legendre.shape
    slots = rows // 4
    radii = curl_map.shape[0] // 8
    out_shape = jax.ShapeDtypeStruct((3, 2, slots_here, radii, degrees), jnp.bfloat16)
    out_spec = pl.BlockSpec((3, 2, 1, radii, degrees), lambda j: (0, 0, base + j, 0, 0))
    return pl.pallas_call(
        functools.partial(legendre_kernel, base, series, lat, degrees),
        grid=(slots,),
        in_specs=[
            pl.BlockSpec(memory_space=pltpu.SMEM),
            pl.BlockSpec(received.shape, lambda j: (0, 0, 0, 0)),
            pl.BlockSpec((1, heights, degrees), lambda j: (base + j, 0, 0)),
            pl.BlockSpec(curl_map.shape, lambda j: (0, 0)),
        ]
        + [pl.BlockSpec(memory_space=pl.ANY)] * len(before),
        out_specs=[out_spec, out_spec],
        out_shape=[out_shape, out_shape],
        input_output_aliases={4 + n: n for n in range(len(before))},
        scratch_shapes=[pltpu.VMEM((slots, 2, 4 * groups * series, heights), jnp.bfloat16)],
        compiler_params=pltpu.CompilerParams(vmem_limit_bytes=56 * 2**20),
        cost_estimate=pl.CostEstimate(
            flops=slots * 2 * 8 * groups * series * heights * degrees * 2,
            bytes_accessed=received.size * 2 + slots * heights * degrees * 2,
            transcendentals=0,
        ),
    )(own_pairs, received, legendre, curl_map, *before)


def direct_path(at_owners, legendre, own_pairs, curl_inputs, potentials, rad_local, lat_local):
    stencil_start, first_weights, second_weights, inv_radius = curl_inputs
    band_count, rows_axis = at_owners.shape[:2]
    slots_here, _, degrees = legendre.shape
    widened = at_owners.astype(jnp.float32).reshape(
        band_count, rows_axis, slots_here, 2, 2, potentials, rad_local, lat_local
    )
    north = widened[: band_count // 2]
    south = jnp.flip(widened[band_count // 2 :], axis=(0, 7))
    folded = jnp.stack([north + south, north - south], axis=0).astype(jnp.bfloat16)
    folded = jnp.transpose(folded, (3, 0, 4, 5, 6, 2, 7, 1, 8)).reshape(
        slots_here, 8 * potentials * rows_axis * rad_local, -1
    )
    product = jnp.einsum("jmh,jhk->jmk", folded, legendre, preferred_element_type=jnp.float32)
    product = product.reshape(slots_here, 2, 2, 2, potentials, rows_axis * rad_local, degrees)
    chosen = select_columns(product, own_pairs, degrees).astype(jnp.bfloat16)
    spectral = jnp.transpose(chosen, (2, 1, 0, 3, 4))
    degree = degree_table(own_pairs, degrees)[2]
    horizontal = ((degree * (degree + 1)).astype(jnp.float32) / (degrees * degrees))[
        None, :, None, :
    ]
    inverse = inv_radius[:, None]
    first_matrix = derivative_matrix(stencil_start, first_weights)
    second_matrix = derivative_matrix(stencil_start, second_weights)
    widened = spectral.astype(jnp.float32)
    current = curl_parts(widened[0], widened[1], first_matrix, second_matrix, horizontal, inverse)
    vorticity = curl_parts(widened[2], widened[3], first_matrix, second_matrix, horizontal, inverse)
    return (current, vorticity)


CHUNKS = 4


def shards(
    grid_fields, pair_list, legendre, stencil_start, first_weights, second_weights, inv_radius
):
    potentials, rad_local, lat_local, points = grid_fields.shape
    degrees = legendre.shape[2]
    slots_here = legendre.shape[0]
    band_count = lax.axis_size("ma")
    rows_axis = lax.axis_size("row")
    series = potentials * rad_local
    flat = grid_fields.reshape(series * lat_local, points)
    device = lax.axis_index("ma") * rows_axis + lax.axis_index("row")
    own_pairs = lax.dynamic_slice_in_dim(pair_list, device * slots_here, slots_here, 0)
    by_owner = pair_list.reshape(-1, slots_here)
    chunks = 1 if lat_local % 128 else math.gcd(CHUNKS, slots_here)
    slots = slots_here // chunks
    curl_inputs = (stencil_start, first_weights, second_weights, inv_radius)
    curl_map = curl_matrix(*curl_inputs, potentials, rows_axis)
    outputs = ()
    for chunk in range(chunks):
        pairs = by_owner[:, chunk * slots : (chunk + 1) * slots].reshape(-1)
        fourier = fourier_table(pairs, degrees, points).reshape(-1, points)
        coefficients = jnp.einsum(
            "mx,nx->mn", fourier, flat, preferred_element_type=jnp.float32
        ).astype(jnp.bfloat16)
        received = lax.all_to_all(
            coefficients, ("ma", "row"), split_axis=0, concat_axis=0, tiled=True
        ).reshape(band_count, rows_axis, 4 * slots, series * lat_local)
        if lat_local % 128:
            return direct_path(
                received, legendre, own_pairs, curl_inputs, potentials, rad_local, lat_local
            )
        outputs = legendre_stage(
            chunk * slots, received, legendre, own_pairs, curl_map, outputs, series, lat_local
        )
    return tuple(outputs)


def solution(mesh):
    in_specs = (P(None, "row", "ma", None), P(), P(("ma", "row"), None, None), P(), P(), P(), P())
    out_specs = (P(None, None, ("ma", "row"), None, None), P(None, None, ("ma", "row"), None, None))
    return jax.shard_map(shards, mesh=mesh, in_specs=in_specs, out_specs=out_specs, check_vma=False)
```

```python
import functools
import math

import jax
import jax.numpy as jnp
from jax import lax
from jax.experimental import pallas as pl
from jax.experimental.pallas import tpu as pltpu
from jax.sharding import PartitionSpec as P


def degree_table(pair_values, degrees):
    column = jnp.arange(degrees, dtype=jnp.int32)
    upper_side = column[None, :] >= (degrees - pair_values)[:, None]
    degree = jnp.where(upper_side, column[None, :], pair_values[:, None] + column[None, :])
    order_value = jnp.where(upper_side, degrees - pair_values[:, None], pair_values[:, None])
    parity = (degree - order_value) % 2
    return (upper_side.astype(jnp.int32), parity, degree)


def fourier_table(pair_values, degrees, points):
    orders = jnp.stack([pair_values, degrees - pair_values], axis=1)
    stride = 128
    factor = 1.0 / math.sqrt(points)

    def waves(positions):
        phases = orders[:, :, None] * positions[None, None, :] % points
        angles = phases.astype(jnp.float32) * (2.0 * math.pi / points)
        return jnp.cos(angles), jnp.sin(angles)

    wide_cos, wide_sin = waves(jnp.arange(points // stride, dtype=jnp.int32) * stride)
    fine_cos, fine_sin = waves(jnp.arange(stride, dtype=jnp.int32))
    wide_cos, wide_sin = wide_cos[..., None] * factor, wide_sin[..., None] * factor
    fine_cos, fine_sin = fine_cos[:, :, None, :], fine_sin[:, :, None, :]
    cosine = wide_cos * fine_cos - wide_sin * fine_sin
    sine = wide_sin * fine_cos + wide_cos * fine_sin
    table = jnp.stack([cosine, -sine], axis=2).astype(jnp.bfloat16)
    return table.reshape(pair_values.shape[0], 4, points)


def derivative_matrix(stencil_start, weights):
    radius_count, stencil_width = weights.shape
    target = stencil_start[:, None] + jnp.arange(stencil_width, dtype=jnp.int32)[None, :]
    matches = target[:, :, None] == jnp.arange(radius_count, dtype=jnp.int32)[None, None, :]
    return jnp.sum(jnp.where(matches, weights[:, :, None], 0.0), axis=1)


def radial(matrix, values):
    return jnp.einsum("rt,cjtk->cjrk", matrix, values, precision=lax.Precision.HIGHEST)


def curl_parts(poloidal, toroidal, first_matrix, second_matrix, horizontal, inverse):
    poloidal_first = radial(first_matrix, poloidal)
    poloidal_second = radial(second_matrix, poloidal)
    toroidal_first = radial(first_matrix, toroidal)
    radial_part = horizontal * inverse * toroidal
    spheroidal = toroidal_first + inverse * toroidal
    toroidal_part = (
        -(poloidal_second + 2.0 * inverse * poloidal_first)
        + horizontal * inverse * inverse * poloidal
    )
    return jnp.stack([radial_part, spheroidal, toroidal_part], axis=0).astype(jnp.bfloat16)


def select_columns(product, pair_values, degrees):
    upper_side, parity, _ = degree_table(pair_values, degrees)
    wide = (slice(None),) + (None,) * 3 + (slice(None),)
    by_side = jnp.where(upper_side[:, None][wide] == 1, product[:, :, 1], product[:, :, 0])
    return jnp.where(parity[wide] == 1, by_side[:, 1], by_side[:, 0])


def curl_matrix(stencil_start, first_weights, second_weights, inv_radius, potentials, groups):
    radii = inv_radius.shape[0]
    first = derivative_matrix(stencil_start, first_weights)
    second = derivative_matrix(stencil_start, second_weights)
    inverse = inv_radius[:, None]
    unit = jnp.eye(radii, dtype=jnp.float32)
    zero = jnp.zeros((radii, radii), jnp.float32)
    on_poloidal = [zero, zero, -(second + 2.0 * inverse * first), inverse * inverse * unit]
    on_toroidal = [inverse * unit, first + inverse * unit, zero, zero]
    pair_map = jnp.stack([jnp.stack(on_poloidal), jnp.stack(on_toroidal)])
    fields = potentials // 2
    whole = jnp.einsum("fe,pkrt->fkrept", jnp.eye(fields, dtype=jnp.float32), pair_map,
                       precision=lax.Precision.HIGHEST)
    whole = whole.reshape(fields * 4 * radii, potentials, groups, radii // groups)
    return jnp.transpose(whole, (0, 2, 1, 3)).reshape(fields * 4 * radii, potentials * radii)


MESH = pl.DeviceIdType.MESH


def fold_chunk(recv_ref, lhs_ref, chunk, bands, groups, series, lat):
    rows = recv_ref.shape[2]
    blocks = groups * series
    flip = (
        lax.broadcasted_iota(jnp.int32, (lat, lat), 0)
        + lax.broadcasted_iota(jnp.int32, (lat, lat), 1)
        == lat - 1
    ).astype(jnp.bfloat16)
    total = blocks * rows
    out_row = lax.broadcasted_iota(jnp.int32, (total, total), 0)
    in_row = lax.broadcasted_iota(jnp.int32, (total, total), 1)
    wanted = (out_row % blocks) * rows + out_row // blocks
    order = (in_row == wanted).astype(jnp.bfloat16)

    def gathered(band):
        pieces = []
        for group in range(groups):
            values = recv_ref[chunk, band * groups + group].astype(jnp.float32)
            pieces += [values[:, n * lat : (n + 1) * lat] for n in range(series)]
        return jnp.concatenate(pieces, axis=0)

    for band in range(bands // 2):
        north = gathered(band)
        south = gathered(bands - 1 - band).astype(jnp.bfloat16)
        south = jnp.dot(south, flip, preferred_element_type=jnp.float32)
        for parity, folded in enumerate((north + south, north - south)):
            lhs_ref[parity, :, band * lat : (band + 1) * lat] = jnp.dot(
                order, folded.astype(jnp.bfloat16), preferred_element_type=jnp.float32
            ).astype(jnp.bfloat16)


def analyse_slot(lhs_ref, first_row, blocks, table_ref, map_ref, q, cur_ref, vor_ref, slot):
    degrees = table_ref.shape[2]
    radii = cur_ref.shape[3]
    width = 256
    for start in range(0, degrees, width):
        columns = slice(start, start + width)
        column = lax.broadcasted_iota(jnp.int32, (1, width), 1) + start
        upper = column >= degrees - q
        degree = jnp.where(upper, column, q + column)
        odd = ((degree - jnp.where(upper, degrees - q, q)) & 1) == 1
        horizontal = (degree * (degree + 1)).astype(jnp.float32) / (degrees * degrees)
        table = table_ref[slot, :, columns]
        even_part, odd_part = [
            jnp.dot(
                lhs_ref[parity, pl.ds(first_row, 4 * blocks)],
                table,
                preferred_element_type=jnp.float32,
            )
            for parity in range(2)
        ]
        chosen = jnp.where(odd, odd_part, even_part)
        chosen = jnp.where(upper, chosen[2 * blocks :], chosen[: 2 * blocks])
        chosen = chosen.astype(jnp.bfloat16).astype(jnp.float32)
        for part in range(2):
            results = jnp.dot(
                map_ref[...],
                chosen[part * blocks : (part + 1) * blocks],
                precision=lax.Precision.HIGHEST,
                preferred_element_type=jnp.float32,
            )
            for field, out_ref in enumerate((cur_ref, vor_ref)):
                kinds = [
                    results[(field * 4 + kind) * radii : (field * 4 + kind + 1) * radii]
                    for kind in range(4)
                ]
                out_ref[0, part, slot, :, columns] = (horizontal * kinds[0]).astype(jnp.bfloat16)
                out_ref[1, part, slot, :, columns] = kinds[1].astype(jnp.bfloat16)
                out_ref[2, part, slot, :, columns] = (kinds[2] + horizontal * kinds[3]).astype(
                    jnp.bfloat16
                )


def exchange_kernel(
    bands, groups, series, lat,
    pairs_ref, fourier_ref, grid_ref, leg_ref, map_ref, cur_ref, vor_ref,
    coef_ref, recv_ref, table_ref, lhs_ref, send_sem, recv_sem, table_sem,
):
    chunks, devices, rows, _ = coef_ref.shape
    slots = rows // 4
    blocks = groups * series
    others = devices - 1
    me = lax.axis_index("ma") * groups + lax.axis_index("row")

    def place(index):
        return (index // groups, index % groups)

    barrier = pltpu.get_barrier_semaphore()

    def greet(k, carry):
        pl.semaphore_signal(
            barrier, inc=1, device_id=place((me + k) % devices), device_id_type=MESH
        )
        return carry

    lax.fori_loop(1, devices, greet, 0)
    pl.semaphore_wait(barrier, others)

    def table_copy(slot):
        return pltpu.make_async_copy(leg_ref.at[slot], table_ref.at[slot], table_sem.at[slot])

    def fetch(slot, carry):
        table_copy(slot).start()
        return carry

    lax.fori_loop(0, chunks * slots, fetch, 0)

    def sent(chunk):
        part = coef_ref.at[chunk, pl.ds(0, others)]
        return pltpu.make_async_copy(part, part, send_sem.at[chunk])

    def arrived(chunk):
        part = recv_ref.at[chunk, pl.ds(0, others)]
        return pltpu.make_async_copy(part, part, recv_sem.at[chunk])

    def transform(chunk, carry):
        orders = fourier_ref[pl.ds(chunk * (devices * rows), devices * rows)]
        for n in range(series):
            values = lax.dot_general(
                orders,
                grid_ref[n * lat : (n + 1) * lat],
                (((1,), (1,)), ((), ())),
                preferred_element_type=jnp.float32,
            )
            coef_ref[chunk, :, :, n * lat : (n + 1) * lat] = values.reshape(
                devices, rows, lat
            ).astype(jnp.bfloat16)

        @pl.when(chunk >= 2)
        def _():
            sent(chunk - 2).wait()

        def send(k, carry):
            target = (me + k) % devices
            pltpu.make_async_remote_copy(
                src_ref=coef_ref.at[chunk, target],
                dst_ref=recv_ref.at[chunk, me],
                send_sem=send_sem.at[chunk],
                recv_sem=recv_sem.at[chunk],
                device_id=place(target),
                device_id_type=MESH,
            ).start()
            return carry

        lax.fori_loop(1, devices, send, 0)
        recv_ref[chunk, me] = coef_ref[chunk, me]
        return carry

    lax.fori_loop(0, chunks, transform, 0)

    def project(chunk, carry):
        arrived(chunk).wait()
        fold_chunk(recv_ref, lhs_ref, chunk, bands, groups, series, lat)

        def one(j, carry):
            slot = chunk * slots + j
            table_copy(slot).wait()
            first_row = pl.multiple_of(j * (4 * blocks), 4 * blocks)
            analyse_slot(
                lhs_ref, first_row, blocks, table_ref, map_ref, pairs_ref[slot], cur_ref, vor_ref,
                slot,
            )
            return carry

        lax.fori_loop(0, slots, one, 0)
        return carry

    lax.fori_loop(0, chunks, project, 0)
    for chunk in range(max(chunks - 2, 0), chunks):
        sent(chunk).wait()


def exchange_stage(fourier, flat, legendre, own_pairs, curl_map, bands, groups, series, chunks):
    slots_here, heights, degrees = legendre.shape
    lat = flat.shape[0] // series
    rows = 4 * slots_here // chunks
    devices = bands * groups
    radii = curl_map.shape[0] // 8
    out_shape = jax.ShapeDtypeStruct((3, 2, slots_here, radii, degrees), jnp.bfloat16)
    vmem = pl.BlockSpec(memory_space=pltpu.VMEM)
    buffer = pltpu.VMEM((chunks, devices, rows, series * lat), jnp.bfloat16)
    return pl.pallas_call(
        functools.partial(exchange_kernel, bands, groups, series, lat),
        in_specs=[
            pl.BlockSpec(memory_space=pltpu.SMEM),
            vmem,
            vmem,
            pl.BlockSpec(memory_space=pl.ANY),
            vmem,
        ],
        out_specs=[vmem, vmem],
        out_shape=[out_shape, out_shape],
        scratch_shapes=[
            buffer,
            buffer,
            pltpu.VMEM(legendre.shape, jnp.bfloat16),
            pltpu.VMEM((2, rows * groups * series, heights), jnp.bfloat16),
            pltpu.SemaphoreType.DMA((chunks,)),
            pltpu.SemaphoreType.DMA((chunks,)),
            pltpu.SemaphoreType.DMA((slots_here,)),
        ],
        compiler_params=pltpu.CompilerParams(
            vmem_limit_bytes=61 * 2**20, collective_id=0, has_side_effects=True
        ),
    )(own_pairs, fourier, flat, legendre, curl_map)


def direct_path(at_owners, legendre, own_pairs, curl_inputs, potentials, rad_local, lat_local):
    stencil_start, first_weights, second_weights, inv_radius = curl_inputs
    band_count, rows_axis = at_owners.shape[:2]
    slots_here, _, degrees = legendre.shape
    widened = at_owners.astype(jnp.float32).reshape(
        band_count, rows_axis, slots_here, 2, 2, potentials, rad_local, lat_local
    )
    north = widened[: band_count // 2]
    south = jnp.flip(widened[band_count // 2 :], axis=(0, 7))
    folded = jnp.stack([north + south, north - south], axis=0).astype(jnp.bfloat16)
    folded = jnp.transpose(folded, (3, 0, 4, 5, 6, 2, 7, 1, 8)).reshape(
        slots_here, 8 * potentials * rows_axis * rad_local, -1
    )
    product = jnp.einsum("jmh,jhk->jmk", folded, legendre, preferred_element_type=jnp.float32)
    product = product.reshape(slots_here, 2, 2, 2, potentials, rows_axis * rad_local, degrees)
    chosen = select_columns(product, own_pairs, degrees).astype(jnp.bfloat16)
    spectral = jnp.transpose(chosen, (2, 1, 0, 3, 4))
    degree = degree_table(own_pairs, degrees)[2]
    horizontal = ((degree * (degree + 1)).astype(jnp.float32) / (degrees * degrees))[
        None, :, None, :
    ]
    inverse = inv_radius[:, None]
    first_matrix = derivative_matrix(stencil_start, first_weights)
    second_matrix = derivative_matrix(stencil_start, second_weights)
    widened = spectral.astype(jnp.float32)
    current = curl_parts(widened[0], widened[1], first_matrix, second_matrix, horizontal, inverse)
    vorticity = curl_parts(widened[2], widened[3], first_matrix, second_matrix, horizontal, inverse)
    return (current, vorticity)


CHUNKS = 4


def shards(
    grid_fields, pair_list, legendre, stencil_start, first_weights, second_weights, inv_radius
):
    potentials, rad_local, lat_local, points = grid_fields.shape
    degrees = legendre.shape[2]
    slots_here = legendre.shape[0]
    band_count = lax.axis_size("ma")
    rows_axis = lax.axis_size("row")
    series = potentials * rad_local
    flat = grid_fields.reshape(series * lat_local, points)
    device = lax.axis_index("ma") * rows_axis + lax.axis_index("row")
    own_pairs = lax.dynamic_slice_in_dim(pair_list, device * slots_here, slots_here, 0)
    curl_inputs = (stencil_start, first_weights, second_weights, inv_radius)
    if lat_local % 128:
        fourier = fourier_table(pair_list, degrees, points).reshape(-1, points)
        coefficients = jnp.einsum(
            "mx,nx->mn", fourier, flat, preferred_element_type=jnp.float32
        ).astype(jnp.bfloat16)
        received = lax.all_to_all(
            coefficients, ("ma", "row"), split_axis=0, concat_axis=0, tiled=True
        ).reshape(band_count, rows_axis, 4 * slots_here, series * lat_local)
        return direct_path(
            received, legendre, own_pairs, curl_inputs, potentials, rad_local, lat_local
        )
    chunks = math.gcd(CHUNKS, slots_here)
    by_chunk = jnp.transpose(pair_list.reshape(-1, chunks, slots_here // chunks), (1, 0, 2))
    fourier = fourier_table(by_chunk.reshape(-1), degrees, points).reshape(-1, points)
    curl_map = curl_matrix(*curl_inputs, potentials, rows_axis)
    return tuple(
        exchange_stage(
            fourier, flat, legendre, own_pairs, curl_map, band_count, rows_axis, series, chunks
        )
    )


def solution(mesh):
    in_specs = (P(None, "row", "ma", None), P(), P(("ma", "row"), None, None), P(), P(), P(), P())
    out_specs = (P(None, None, ("ma", "row"), None, None), P(None, None, ("ma", "row"), None, None))
    return jax.shard_map(shards, mesh=mesh, in_specs=in_specs, out_specs=out_specs, check_vma=False)
```

```python
import functools
import math

import jax
import jax.numpy as jnp
from jax import lax
from jax.experimental import pallas as pl
from jax.experimental.pallas import tpu as pltpu
from jax.sharding import PartitionSpec as P


def degree_table(pair_values, degrees):
    column = jnp.arange(degrees, dtype=jnp.int32)
    upper_side = column[None, :] >= (degrees - pair_values)[:, None]
    degree = jnp.where(upper_side, column[None, :], pair_values[:, None] + column[None, :])
    order_value = jnp.where(upper_side, degrees - pair_values[:, None], pair_values[:, None])
    parity = (degree - order_value) % 2
    return (upper_side.astype(jnp.int32), parity, degree)


def fourier_table(pair_values, degrees, points):
    orders = jnp.stack([pair_values, degrees - pair_values], axis=1)
    stride = 128
    factor = 1.0 / math.sqrt(points)

    def waves(positions):
        phases = orders[:, :, None] * positions[None, None, :] % points
        angles = phases.astype(jnp.float32) * (2.0 * math.pi / points)
        return jnp.cos(angles), jnp.sin(angles)

    wide_cos, wide_sin = waves(jnp.arange(points // stride, dtype=jnp.int32) * stride)
    fine_cos, fine_sin = waves(jnp.arange(stride, dtype=jnp.int32))
    wide_cos, wide_sin = wide_cos[..., None] * factor, wide_sin[..., None] * factor
    fine_cos, fine_sin = fine_cos[:, :, None, :], fine_sin[:, :, None, :]
    cosine = wide_cos * fine_cos - wide_sin * fine_sin
    sine = wide_sin * fine_cos + wide_cos * fine_sin
    table = jnp.stack([cosine, -sine], axis=2).astype(jnp.bfloat16)
    return table.reshape(pair_values.shape[0], 4, points)


def derivative_matrix(stencil_start, weights):
    radius_count, stencil_width = weights.shape
    target = stencil_start[:, None] + jnp.arange(stencil_width, dtype=jnp.int32)[None, :]
    matches = target[:, :, None] == jnp.arange(radius_count, dtype=jnp.int32)[None, None, :]
    return jnp.sum(jnp.where(matches, weights[:, :, None], 0.0), axis=1)


def radial(matrix, values):
    return jnp.einsum("rt,cjtk->cjrk", matrix, values, precision=lax.Precision.HIGHEST)


def curl_parts(poloidal, toroidal, first_matrix, second_matrix, horizontal, inverse):
    poloidal_first = radial(first_matrix, poloidal)
    poloidal_second = radial(second_matrix, poloidal)
    toroidal_first = radial(first_matrix, toroidal)
    radial_part = horizontal * inverse * toroidal
    spheroidal = toroidal_first + inverse * toroidal
    toroidal_part = (
        -(poloidal_second + 2.0 * inverse * poloidal_first)
        + horizontal * inverse * inverse * poloidal
    )
    return jnp.stack([radial_part, spheroidal, toroidal_part], axis=0).astype(jnp.bfloat16)


def select_columns(product, pair_values, degrees):
    upper_side, parity, _ = degree_table(pair_values, degrees)
    wide = (slice(None),) + (None,) * 3 + (slice(None),)
    by_side = jnp.where(upper_side[:, None][wide] == 1, product[:, :, 1], product[:, :, 0])
    return jnp.where(parity[wide] == 1, by_side[:, 1], by_side[:, 0])


def curl_matrix(stencil_start, first_weights, second_weights, inv_radius, potentials, groups):
    radii = inv_radius.shape[0]
    first = derivative_matrix(stencil_start, first_weights)
    second = derivative_matrix(stencil_start, second_weights)
    inverse = inv_radius[:, None]
    unit = jnp.eye(radii, dtype=jnp.float32)
    zero = jnp.zeros((radii, radii), jnp.float32)
    on_poloidal = [zero, zero, -(second + 2.0 * inverse * first), inverse * inverse * unit]
    on_toroidal = [inverse * unit, first + inverse * unit, zero, zero]
    pair_map = jnp.stack([jnp.stack(on_poloidal), jnp.stack(on_toroidal)])
    fields = potentials // 2
    whole = jnp.einsum("fe,pkrt->fkrept", jnp.eye(fields, dtype=jnp.float32), pair_map,
                       precision=lax.Precision.HIGHEST)
    whole = whole.reshape(fields * 4 * radii, potentials, groups, radii // groups)
    return jnp.transpose(whole, (0, 2, 1, 3)).reshape(fields * 4 * radii, potentials * radii)


MESH = pl.DeviceIdType.MESH


def fixed_matrices(flip_ref, order_ref, blocks):
    lat, total = flip_ref.shape[0], order_ref.shape[0]
    rows = total // blocks
    flip_ref[...] = (
        lax.broadcasted_iota(jnp.int32, (lat, lat), 0)
        + lax.broadcasted_iota(jnp.int32, (lat, lat), 1)
        == lat - 1
    ).astype(jnp.bfloat16)
    out_row = lax.broadcasted_iota(jnp.int32, (total, 1), 0)
    in_row = lax.broadcasted_iota(jnp.int32, (total, total), 1)
    wanted = (out_row % blocks) * rows + out_row // blocks
    order_ref[...] = (in_row == wanted).astype(jnp.bfloat16)


def fourier_chunk(pairs_ref, table_ref, chunk, slots_here, slots, degrees):
    total, points = table_ref.shape
    pairs_all = pairs_ref.shape[1]
    stride = 128
    row = lax.broadcasted_iota(jnp.int32, (total, 1), 0)
    wanted = row // (4 * slots) * slots_here + chunk * slots + row // 4 % slots
    slot = lax.broadcasted_iota(jnp.int32, (total, pairs_all), 1)
    listed = jnp.where(slot == wanted, pairs_ref[...].astype(jnp.float32), 0.0)
    q = jnp.sum(listed, axis=1, keepdims=True).astype(jnp.int32)
    order_value = jnp.where(row // 2 % 2 == 1, degrees - q, q)
    imaginary = row % 2 == 1
    lane = lax.broadcasted_iota(jnp.int32, (total, stride), 1)

    def waves(positions):
        turns = order_value * positions
        phases = turns % points if points & (points - 1) else turns & (points - 1)
        angles = phases.astype(jnp.float32) * (2.0 * math.pi / points)
        return jnp.cos(angles), jnp.sin(angles)

    fine_cos, fine_sin = waves(lane)
    wide_cos, wide_sin = waves(lane % (points // stride) * stride)
    factor = 1.0 / math.sqrt(points)
    on_cos = jnp.where(imaginary, -wide_sin, wide_cos) * factor
    on_sin = jnp.where(imaginary, wide_cos, wide_sin) * factor
    for part in range(points // stride):
        entries = on_cos[:, part : part + 1] * fine_cos - on_sin[:, part : part + 1] * fine_sin
        table_ref[:, part * stride : (part + 1) * stride] = entries.astype(jnp.bfloat16)


def fold_chunk(recv_ref, lhs_ref, flip, order, chunk, bands, groups, series, lat):
    def gathered(band):
        pieces = []
        for group in range(groups):
            values = recv_ref[chunk, band * groups + group].astype(jnp.float32)
            pieces += [values[:, n * lat : (n + 1) * lat] for n in range(series)]
        return jnp.concatenate(pieces, axis=0)

    for band in range(bands // 2):
        north = gathered(band)
        south = gathered(bands - 1 - band).astype(jnp.bfloat16)
        south = jnp.dot(south, flip, preferred_element_type=jnp.float32)
        for parity, folded in enumerate((north + south, north - south)):
            lhs_ref[parity, :, band * lat : (band + 1) * lat] = jnp.dot(
                order, folded.astype(jnp.bfloat16), preferred_element_type=jnp.float32
            ).astype(jnp.bfloat16)


def analyse_slot(lhs_ref, first_row, blocks, table_ref, map_ref, q, cur_ref, vor_ref, slot):
    degrees = table_ref.shape[2]
    radii = cur_ref.shape[3]
    width = 256
    for start in range(0, degrees, width):
        columns = slice(start, start + width)
        column = lax.broadcasted_iota(jnp.int32, (1, width), 1) + start
        upper = column >= degrees - q
        degree = jnp.where(upper, column, q + column)
        odd = ((degree - jnp.where(upper, degrees - q, q)) & 1) == 1
        horizontal = (degree * (degree + 1)).astype(jnp.float32) / (degrees * degrees)
        table = table_ref[slot, :, columns]
        even_part, odd_part = [
            jnp.dot(
                lhs_ref[parity, pl.ds(first_row, 4 * blocks)],
                table,
                preferred_element_type=jnp.float32,
            )
            for parity in range(2)
        ]
        chosen = jnp.where(odd, odd_part, even_part)
        chosen = jnp.where(upper, chosen[2 * blocks :], chosen[: 2 * blocks])
        chosen = chosen.astype(jnp.bfloat16).astype(jnp.float32)
        for part in range(2):
            results = jnp.dot(
                map_ref[...],
                chosen[part * blocks : (part + 1) * blocks],
                precision=lax.Precision.HIGHEST,
                preferred_element_type=jnp.float32,
            )
            for field, out_ref in enumerate((cur_ref, vor_ref)):
                kinds = [
                    results[(field * 4 + kind) * radii : (field * 4 + kind + 1) * radii]
                    for kind in range(4)
                ]
                out_ref[0, part, slot, :, columns] = (horizontal * kinds[0]).astype(jnp.bfloat16)
                out_ref[1, part, slot, :, columns] = kinds[1].astype(jnp.bfloat16)
                out_ref[2, part, slot, :, columns] = (kinds[2] + horizontal * kinds[3]).astype(
                    jnp.bfloat16
                )


def exchange_kernel(
    bands, groups, series, lat,
    pairs_ref, list_ref, fields_ref, leg_ref, map_ref, cur_ref, vor_ref,
    coef_ref, recv_ref, table_ref, lhs_ref, grid_ref, fourier_ref, flip_ref, order_ref,
    send_sem, recv_sem, table_sem, grid_sem,
):
    chunks, devices, rows, _ = coef_ref.shape
    slots = rows // 4
    blocks = groups * series
    others = devices - 1
    me = lax.axis_index("ma") * groups + lax.axis_index("row")

    def place(index):
        return (index // groups, index % groups)

    barrier = pltpu.get_barrier_semaphore()

    def greet(k, carry):
        pl.semaphore_signal(
            barrier, inc=1, device_id=place((me + k) % devices), device_id_type=MESH
        )
        return carry

    lax.fori_loop(1, devices, greet, 0)

    def grid_copy(n):
        part = pl.ds(n * lat, lat)
        return pltpu.make_async_copy(fields_ref.at[part], grid_ref.at[part], grid_sem.at[n])

    for n in range(series):
        grid_copy(n).start()
    pl.semaphore_wait(barrier, others)

    def table_copy(slot):
        return pltpu.make_async_copy(leg_ref.at[slot], table_ref.at[slot], table_sem.at[slot])

    def fetch(slot, carry):
        table_copy(slot).start()
        return carry

    def sent(chunk):
        part = coef_ref.at[chunk, pl.ds(0, others)]
        return pltpu.make_async_copy(part, part, send_sem.at[chunk])

    def arrived(chunk):
        part = recv_ref.at[chunk, pl.ds(0, others)]
        return pltpu.make_async_copy(part, part, recv_sem.at[chunk])

    def transform(chunk, carry):
        fourier_chunk(
            list_ref, fourier_ref, chunk, chunks * slots, slots, leg_ref.shape[2]
        )
        for n in range(series):

            @pl.when(chunk == 0)
            def _():
                grid_copy(n).wait()

            values = lax.dot_general(
                fourier_ref[...],
                grid_ref[n * lat : (n + 1) * lat],
                (((1,), (1,)), ((), ())),
                preferred_element_type=jnp.float32,
            )
            coef_ref[chunk, :, :, n * lat : (n + 1) * lat] = values.reshape(
                devices, rows, lat
            ).astype(jnp.bfloat16)

        @pl.when(chunk >= 2)
        def _():
            sent(chunk - 2).wait()

        def send(k, carry):
            target = (me + k) % devices
            pltpu.make_async_remote_copy(
                src_ref=coef_ref.at[chunk, target],
                dst_ref=recv_ref.at[chunk, me],
                send_sem=send_sem.at[chunk],
                recv_sem=recv_sem.at[chunk],
                device_id=place(target),
                device_id_type=MESH,
            ).start()
            return carry

        lax.fori_loop(1, devices, send, 0)
        recv_ref[chunk, me] = coef_ref[chunk, me]

        @pl.when(chunk == 0)
        def _():
            lax.fori_loop(0, chunks * slots, fetch, 0)

        return carry

    lax.fori_loop(0, chunks, transform, 0)
    fixed_matrices(flip_ref, order_ref, blocks)

    def project(chunk, carry):
        arrived(chunk).wait()
        fold_chunk(
            recv_ref, lhs_ref, flip_ref[...], order_ref[...], chunk, bands, groups, series, lat
        )

        def one(j, carry):
            slot = chunk * slots + j
            table_copy(slot).wait()
            first_row = pl.multiple_of(j * (4 * blocks), 4 * blocks)
            analyse_slot(
                lhs_ref, first_row, blocks, table_ref, map_ref,
                pairs_ref[me * (chunks * slots) + slot], cur_ref, vor_ref, slot,
            )
            return carry

        lax.fori_loop(0, slots, one, 0)
        return carry

    lax.fori_loop(0, chunks, project, 0)
    for chunk in range(max(chunks - 2, 0), chunks):
        sent(chunk).wait()


def exchange_stage(pair_list, flat, legendre, curl_map, bands, groups, series, chunks):
    slots_here, heights, degrees = legendre.shape
    lat = flat.shape[0] // series
    rows = 4 * slots_here // chunks
    devices = bands * groups
    radii = curl_map.shape[0] // 8
    out_shape = jax.ShapeDtypeStruct((3, 2, slots_here, radii, degrees), jnp.bfloat16)
    vmem = pl.BlockSpec(memory_space=pltpu.VMEM)
    buffer = pltpu.VMEM((chunks, devices, rows, series * lat), jnp.bfloat16)
    return pl.pallas_call(
        functools.partial(exchange_kernel, bands, groups, series, lat),
        in_specs=[
            pl.BlockSpec(memory_space=pltpu.SMEM),
            vmem,
            pl.BlockSpec(memory_space=pl.ANY),
            pl.BlockSpec(memory_space=pl.ANY),
            vmem,
        ],
        out_specs=[vmem, vmem],
        out_shape=[out_shape, out_shape],
        scratch_shapes=[
            buffer,
            buffer,
            pltpu.VMEM(legendre.shape, jnp.bfloat16),
            pltpu.VMEM((2, rows * groups * series, heights), jnp.bfloat16),
            pltpu.VMEM(flat.shape, jnp.bfloat16),
            pltpu.VMEM((devices * rows, flat.shape[1]), jnp.bfloat16),
            pltpu.VMEM((lat, lat), jnp.bfloat16),
            pltpu.VMEM((rows * groups * series,) * 2, jnp.bfloat16),
            pltpu.SemaphoreType.DMA((chunks,)),
            pltpu.SemaphoreType.DMA((chunks,)),
            pltpu.SemaphoreType.DMA((slots_here,)),
            pltpu.SemaphoreType.DMA((series,)),
        ],
        compiler_params=pltpu.CompilerParams(
            vmem_limit_bytes=61 * 2**20, collective_id=0, has_side_effects=True
        ),
    )(pair_list, pair_list.reshape(1, -1), flat, legendre, curl_map)


def direct_path(at_owners, legendre, own_pairs, curl_inputs, potentials, rad_local, lat_local):
    stencil_start, first_weights, second_weights, inv_radius = curl_inputs
    band_count, rows_axis = at_owners.shape[:2]
    slots_here, _, degrees = legendre.shape
    widened = at_owners.astype(jnp.float32).reshape(
        band_count, rows_axis, slots_here, 2, 2, potentials, rad_local, lat_local
    )
    north = widened[: band_count // 2]
    south = jnp.flip(widened[band_count // 2 :], axis=(0, 7))
    folded = jnp.stack([north + south, north - south], axis=0).astype(jnp.bfloat16)
    folded = jnp.transpose(folded, (3, 0, 4, 5, 6, 2, 7, 1, 8)).reshape(
        slots_here, 8 * potentials * rows_axis * rad_local, -1
    )
    product = jnp.einsum("jmh,jhk->jmk", folded, legendre, preferred_element_type=jnp.float32)
    product = product.reshape(slots_here, 2, 2, 2, potentials, rows_axis * rad_local, degrees)
    chosen = select_columns(product, own_pairs, degrees).astype(jnp.bfloat16)
    spectral = jnp.transpose(chosen, (2, 1, 0, 3, 4))
    degree = degree_table(own_pairs, degrees)[2]
    horizontal = ((degree * (degree + 1)).astype(jnp.float32) / (degrees * degrees))[
        None, :, None, :
    ]
    inverse = inv_radius[:, None]
    first_matrix = derivative_matrix(stencil_start, first_weights)
    second_matrix = derivative_matrix(stencil_start, second_weights)
    widened = spectral.astype(jnp.float32)
    current = curl_parts(widened[0], widened[1], first_matrix, second_matrix, horizontal, inverse)
    vorticity = curl_parts(widened[2], widened[3], first_matrix, second_matrix, horizontal, inverse)
    return (current, vorticity)


CHUNKS = 4


def shards(
    grid_fields, pair_list, legendre, stencil_start, first_weights, second_weights, inv_radius
):
    potentials, rad_local, lat_local, points = grid_fields.shape
    degrees = legendre.shape[2]
    slots_here = legendre.shape[0]
    band_count = lax.axis_size("ma")
    rows_axis = lax.axis_size("row")
    series = potentials * rad_local
    flat = grid_fields.reshape(series * lat_local, points)
    device = lax.axis_index("ma") * rows_axis + lax.axis_index("row")
    own_pairs = lax.dynamic_slice_in_dim(pair_list, device * slots_here, slots_here, 0)
    curl_inputs = (stencil_start, first_weights, second_weights, inv_radius)
    if lat_local % 128:
        fourier = fourier_table(pair_list, degrees, points).reshape(-1, points)
        coefficients = jnp.einsum(
            "mx,nx->mn", fourier, flat, preferred_element_type=jnp.float32
        ).astype(jnp.bfloat16)
        received = lax.all_to_all(
            coefficients, ("ma", "row"), split_axis=0, concat_axis=0, tiled=True
        ).reshape(band_count, rows_axis, 4 * slots_here, series * lat_local)
        return direct_path(
            received, legendre, own_pairs, curl_inputs, potentials, rad_local, lat_local
        )
    chunks = math.gcd(CHUNKS, slots_here)
    curl_map = curl_matrix(*curl_inputs, potentials, rows_axis)
    return tuple(
        exchange_stage(
            pair_list, flat, legendre, curl_map, band_count, rows_axis, series, chunks
        )
    )


def solution(mesh):
    in_specs = (P(None, "row", "ma", None), P(), P(("ma", "row"), None, None), P(), P(), P(), P())
    out_specs = (P(None, None, ("ma", "row"), None, None), P(None, None, ("ma", "row"), None, None))
    return jax.shard_map(shards, mesh=mesh, in_specs=in_specs, out_specs=out_specs, check_vma=False)
```
